32 devices in a mesh: tiles: 2 (over x), disp: 8 (over z, y), rows: 2 (over core).
Axes of the slice: x: 2, y: 2, z: 4, core: 2. Of those that a mesh axis runs over, the one named last changes fastest.
Arguments:
- volume: bfloat16 [32, 192, 64, 512], P(None, 'disp', ('tiles', 'rows')), parts along dimension 2, may hold values from -1000 to 1000, as said below
- conv_weight: bfloat16 [27, 32, 32], replicated, may hold values from -0.21875 to 0.21875
- conv_bias: float32 [32], replicated, may hold values from -3 to 3
- reg_weight: bfloat16 [27, 32], replicated, may hold values from -0.875 to 0.875
Outputs:
- disparity: float32 [64, 512], P(('tiles', 'rows')), parts along dimension 0
The draws below stay inside these ranges and needn't reach their ends.
There are 2 independent parts, one for each index of `tiles`. The reference program is written for one: setup_inputs(seed, part) draws one part's arguments, and reference() takes and returns one part's arrays. A program takes and returns all parts, laid end to end along the dimension named above; an argument that names none is the same for every part. Nothing has to cross between parts.
Inputs may be any that keep to these rules, and one draw needn't show every extreme that they name: `volume`: Real-valued matching features.
All inputs are finite; a program needn't handle non-finite values.
Results may differ from the reference program's by a relative error of at most 0.008.
Values may be sent and summed in bfloat16 or wider, within the bound.
A program may use at most 384 MiB of HBM per device.

```python
import jax
import jax.numpy as jnp
from jax import lax

CH = 32
DISP = 192
WIDTH = 512
ROWS = 32


def draw_volume(key, part):
    first = jax.random.fold_in(jax.random.fold_in(key, 7), 0)
    base = jnp.clip(jax.random.normal(first, (CH, DISP, ROWS, WIDTH), jnp.float32), -6.0, 6.0)
    return base.astype(jnp.bfloat16)


def bell_draw(key, dims, deviation, limit, held_as=jnp.bfloat16):
    drawn = deviation * jax.random.normal(key, dims, jnp.float32)
    return jnp.clip(drawn, min=-limit, max=limit).astype(held_as)


def setup_inputs(seed: int = 0, part: int = 0) -> dict:
    splits = jax.random.split(jax.random.key(seed), 5)
    part_splits = jax.random.split(jax.random.fold_in(splits[4], part), 5)
    volume = draw_volume(jax.random.fold_in(jax.random.fold_in(splits[4], part), 71), part)
    conv_weight = bell_draw(splits[1], (27, CH, CH), (27 * CH) ** -0.5, 0.21875)
    conv_bias = bell_draw(splits[2], (CH,), 0.5, 3.0, jnp.float32)
    reg_weight = bell_draw(splits[3], (27, CH), (27 * CH // 16) ** -0.5, 0.875)
    return {"volume": volume, "conv_weight": conv_weight, "conv_bias": conv_bias, "reg_weight": reg_weight}


def aggregate(volume, conv_weight, conv_bias):
    padded = jnp.pad(volume, ((0, 0), (1, 1), (1, 1), (1, 1))).astype(jnp.float32)
    weights = conv_weight.astype(jnp.float32)
    summed = jnp.zeros((CH, DISP, ROWS, WIDTH), jnp.float32)
    for depth_tap in range(3):
        for row_tap in range(3):
            for col_tap in range(3):
                window = padded[:, depth_tap:depth_tap + DISP, row_tap:row_tap + ROWS, col_tap:col_tap + WIDTH]
                summed = summed + jnp.einsum("oc,cdhw->odhw", weights[9 * depth_tap + 3 * row_tap + col_tap], window, precision=lax.Precision.HIGHEST)
    return jnp.maximum(summed + conv_bias[:, None, None, None], 0.0).astype(jnp.bfloat16)


def regress(hidden, reg_weight):
    padded = jnp.pad(hidden, ((0, 0), (1, 1), (1, 1), (1, 1))).astype(jnp.float32)
    weights = reg_weight.astype(jnp.float32)
    cost = jnp.zeros((DISP, ROWS, WIDTH), jnp.float32)
    for depth_tap in range(3):
        for row_tap in range(3):
            for col_tap in range(3):
                window = padded[:, depth_tap:depth_tap + DISP, row_tap:row_tap + ROWS, col_tap:col_tap + WIDTH]
                cost = cost + jnp.einsum("c,cdhw->dhw", weights[9 * depth_tap + 3 * row_tap + col_tap], window, precision=lax.Precision.HIGHEST)
    return cost


def reference(volume, conv_weight, conv_bias, reg_weight):
    hidden = aggregate(volume, conv_weight, conv_bias)
    cost = regress(hidden, reg_weight)
    score = -cost
    peak = jnp.max(score, axis=0)
    expo = jnp.exp(score - peak[None])
    planes = jnp.arange(DISP).astype(jnp.float32)
    total = jnp.sum(expo, axis=0)
    moment = jnp.sum(planes[:, None, None] * expo, axis=0)
    return moment / total
```

```python
import functools

import jax
import jax.numpy as jnp
from jax import lax
from jax.experimental import pallas as pl
from jax.experimental.pallas import tpu as pltpu
from jax.sharding import PartitionSpec as P

BF = jnp.bfloat16
F32 = jnp.float32
MESH = pl.DeviceIdType.MESH
LANES = 128


def combine(first, second):
    peak = jnp.maximum(first[0], second[0])
    left = jnp.exp(first[0] - peak)
    right = jnp.exp(second[0] - peak)
    return jnp.stack((peak, first[1] * left + second[1] * right, first[2] * left + second[2] * right))


def joined(value, axis):
    count = lax.axis_size(axis)
    if count & (count - 1):
        pieces = lax.all_gather(value, axis)
        running = pieces[0]
        for i in range(1, count):
            running = combine(running, pieces[i])
        return running
    step = 1
    while step < count:
        other = lax.ppermute(value, axis, [(i, i ^ step) for i in range(count)])
        value = combine(value, other)
        step *= 2
    return value


def moved(x, step):
    width = x.shape[1]
    rolled = pltpu.roll(x, step % width, 1)
    lane = lax.broadcasted_iota(jnp.int32, x.shape, 1)
    return jnp.where(lane == (0 if step == 1 else width - 1), jnp.zeros((), x.dtype), rolled)


def fill_a(cw, a_ref):
    ch = cw.shape[1]
    empty = jnp.zeros((ch, ch), F32)
    for a in range(3):
        for c in range(3):
            taps = [cw[9 * a + 3 * b + c].astype(F32) for b in range(3)]
            for r in range(2):
                parts = [taps[s - r] if 0 <= s - r < 3 else empty for s in range(4)]
                block = jnp.concatenate(parts, axis=1).astype(BF)
                for p in range(2):
                    col = ((a + p) * 3 + c) * 4 * ch
                    row = (2 * p + r) * ch
                    a_ref[row : row + ch, col : col + 4 * ch] = block
    zero = jnp.zeros((2 * ch, 12 * ch), BF)
    a_ref[: 2 * ch, 36 * ch :] = zero
    a_ref[2 * ch :, : 12 * ch] = zero


def fill_r(rw, r_ref, height, side):
    ch = rw.shape[1]
    span = 4 * ch
    lane = lax.broadcasted_iota(jnp.int32, (height, span), 1)
    odd = (lane // ch) % 2
    row = lax.broadcasted_iota(jnp.int32, (height, span), 0)
    lane8 = lax.broadcasted_iota(jnp.int32, (8, span), 1)
    odd8 = (lane8 // ch) % 2
    row8 = lax.broadcasted_iota(jnp.int32, (8, span), 0)
    empty = jnp.zeros((1, 2 * ch), F32)

    def line(q, c, b):
        parts = []
        for p in range(2):
            a = p - q + 2
            if 0 <= a < 3:
                t = 9 * a + 3 * b + c
                w = rw[t : t + 1, :].astype(F32)
                parts += [w, w]
            else:
                parts.append(empty)
        return jnp.concatenate(parts, axis=1)

    count = height // 2
    for c in range(3):
        edge_low = jnp.zeros((8, span), F32)
        edge_high = jnp.zeros((8, span), F32)
        for q in range(4):
            lines = [line(q, c, b) for b in range(3)]
            base = (3 * q + c) * height
            for j in range(count):
                place = 2 * j + odd + 1 - row
                out = jnp.zeros((height, span), F32)
                for b in range(3):
                    out = jnp.where(place == b, lines[b], out)
                r_ref[base : base + height, span * j : span * (j + 1)] = out.astype(BF)
            edge_low = jnp.where((row8 == q) & (odd8 == 0), lines[2], edge_low)
            edge_high = jnp.where((row8 == q) & (odd8 == 1), lines[0], edge_high)
        base = 12 * height + 8 * c
        low = jnp.where(side == 1, edge_low, 0.0)
        high = jnp.where(side == 0, edge_high, 0.0)
        for j in range(count):
            value = jnp.zeros((8, span), F32)
            if j == 0:
                value = value + low
            if j == count - 1:
                value = value + high
            r_ref[base : base + 8, span * j : span * (j + 1)] = value.astype(BF)


def main_kernel(
    whole, vol, cw, cb, rw, out, vbuf, tb, x0, x1, x2, hid, sline, hal, a_ref, r_ref, bias, acc, exst, exin, exdiag,
    prev, following, stats, taken, final, vsem, hsem, lsem, esem, csem, each,
):
    ch, planes, height, width = vol.shape
    pairs = planes // 2
    inner = pairs - 2
    windows = height // 2
    n = lax.axis_size("disp")
    me = lax.axis_index("disp")
    r = lax.axis_index("rows")
    up = jnp.minimum(me + 1, n - 1)
    down = jnp.maximum(me - 1, 0)
    xs = (x0, x1)

    def send(src, dst, sems, index, where):
        return pltpu.make_async_remote_copy(
            src_ref=src,
            dst_ref=dst,
            send_sem=sems.at[0, index],
            recv_sem=sems.at[1, index],
            device_id=where,
            device_id_type=MESH,
        )

    def load(p):
        return pltpu.make_async_copy(vol.at[:, p], vbuf.at[p + 1], vsem.at[p])

    load(planes - 1).start()
    load(0).start()

    def start_load(p, carry):
        load(p).start()
        return carry

    lax.fori_loop(1, planes - 1, start_load, 0)

    barrier = pltpu.get_barrier_semaphore()
    pl.semaphore_signal(barrier, inc=1, device_id={"rows": 1 - r}, device_id_type=MESH)
    for j in range(1, n):
        pl.semaphore_signal(barrier, inc=1, device_id={"disp": lax.rem(me + j, n)}, device_id_type=MESH)
    for j in (1, n - 1):
        where = {"disp": lax.rem(me + j, n), "rows": 1 - r}
        pl.semaphore_signal(barrier, inc=1, device_id=where, device_id_type=MESH)
    pl.semaphore_wait(barrier, n + 2)

    raw_up = send(vol.at[:, planes - 1], vbuf.at[0], hsem, 0, {"disp": up})
    raw_down = send(vol.at[:, 0], vbuf.at[planes + 1], hsem, 1, {"disp": down})

    @pl.when(me < n - 1)
    def _():
        raw_up.start()

    @pl.when(me > 0)
    def _():
        raw_down.start()

    fill_a(cw, a_ref)
    fill_r(rw, r_ref, height, r)
    bias[...] = jnp.concatenate([jnp.broadcast_to(cb[...], (ch, LANES))] * 4, axis=0)
    acc[...] = jnp.zeros_like(acc)

    @pl.when(me == 0)
    def _():
        vbuf[0] = jnp.zeros((ch, height, width), BF)
        hal[0] = jnp.zeros((ch, width), BF)

    @pl.when(me == n - 1)
    def _():
        vbuf[planes + 1] = jnp.zeros((ch, height, width), BF)
        hal[planes + 1] = jnp.zeros((ch, width), BF)

    tb[2 * pairs + 1] = jnp.zeros((height, ch, width), BF)

    across = width // LANES
    edge = (height - 1) * (1 - r)

    def turn_part(index, part):
        cols = slice(part * LANES, (part + 1) * LANES)
        tb[index, :, :, cols] = jnp.swapaxes(vbuf[index, :, :, cols], 0, 1)

    def turn(index):
        for part in range(across):
            turn_part(index, part)

    far = {"disp": up, "rows": 1 - r}
    near = {"disp": down, "rows": 1 - r}
    last_line = send(sline.at[planes], hal.at[planes], lsem, pairs, {"rows": 1 - r})
    first_line = send(sline.at[1], hal.at[1], lsem, 0, {"rows": 1 - r})
    last_far = send(sline.at[planes], hal.at[0], lsem, pairs + 1, far)
    first_near = send(sline.at[1], hal.at[planes + 1], lsem, pairs + 2, near)

    load(planes - 1).wait()
    load(0).wait()
    for index in (planes, 1):
        turn(index)
        sline[index] = tb[index, edge]
    last_line.start()
    first_line.start()

    @pl.when(me < n - 1)
    def _():
        last_far.start()

    @pl.when(me > 0)
    def _():
        first_near.start()

    def lines(s):
        both = pl.ds(2 * s, 2)
        return send(sline.at[both], hal.at[both], lsem, s, {"rows": 1 - r})

    def post(s):
        for f in range(2):
            sline[2 * s + f] = tb[2 * s + f, edge]
        lines(s).start()

    def await_pair(s):
        load(2 * s - 1).wait()
        load(2 * s).wait()

    def early(s, carry):
        await_pair(s)
        for f in range(2):
            turn(2 * s + f)
        post(s)
        return carry

    lead = min(4, pairs - 1)
    lax.fori_loop(1, lead + 1, early, 0)

    def put_row(x, f, index, line):
        if line == 0:
            value = hal[index]
            value = jnp.where(r == 1, value, jnp.zeros_like(value))
        elif line == height + 1:
            value = hal[index]
            value = jnp.where(r == 0, value, jnp.zeros_like(value))
        else:
            value = tb[index, line - 1]
        at = slice(line * ch, (line + 1) * ch)
        x[f, 0, at, :] = moved(value, 1)
        x[f, 1, at, :] = value
        x[f, 2, at, :] = moved(value, -1)

    def put_rows(x, s, lines_):
        for line in lines_:
            for f in range(2):
                put_row(x, f, 2 * s + f, line)

    def product(k, low, high, between):
        for j in range(windows):
            rows = slice(2 * j * ch, (2 * j + 4) * ch)
            x = jnp.concatenate([x[f, c, rows, :] for x in (low, high) for f in range(2) for c in range(3)], axis=0)
            pre = jnp.dot(a_ref[...], x, preferred_element_type=F32) + jnp.tile(bias[...], (1, across))
            hid[4 * ch * j : 4 * ch * (j + 1), :] = jnp.maximum(pre, 0.0).astype(BF)
            between(j)
        part = jnp.dot(r_ref[...], hid[...], preferred_element_type=F32)

        def gathered(base, step, size):
            one, two, three = (part[base + step * c : base + step * c + size] for c in range(3))
            return moved(one, 1) + two + moved(three, -1)

        for q in range(4):
            acc[2 * k + q] += gathered(3 * q * height, height, height)
        exst[k] = gathered(12 * height, 8, 8)

    def extra(k):
        return send(exst.at[k], exin.at[k], esem, k, {"rows": 1 - r})

    last_line.wait_recv()
    first_line.wait_recv()

    @pl.when(me > 0)
    def _():
        last_far.wait_recv()

    @pl.when(me < n - 1)
    def _():
        first_near.wait_recv()

    for s in range(1, min(2, pairs - 1) + 1):
        lines(s).wait_recv()
        put_rows(xs[s - 1], s, range(height + 2))

    def step(i, parity):
        low, high = xs[parity], xs[1 - parity]
        ahead = jnp.minimum(i + lead + 1, pairs - 1)

        @pl.when(i + lead + 1 < pairs)
        def _():
            await_pair(ahead)

        @pl.when(i + 3 < pairs)
        def _():
            lines(i + 3).wait_recv()

        parts = [(f, part) for f in range(2) for part in range(across)]

        def between(j):
            top = height + 2 if j == windows - 1 else 2 * j + 2
            put_rows(low, i + 3, range(2 * j, top))
            for f, part in parts[j * len(parts) // windows : (j + 1) * len(parts) // windows]:
                turn_part(2 * ahead + f, part)

        product(i + 1, low, high, between)

        @pl.when(i + lead + 1 < pairs)
        def _():
            post(ahead)

        extra(i + 1).start()

    def two(t, carry):
        step(2 * t, 0)
        step(2 * t + 1, 1)
        return carry

    lax.fori_loop(0, inner // 2, two, 0)
    if inner % 2:
        step(inner - 1, 0)
    high, low = xs[(inner + 1) % 2], xs[inner % 2]

    @pl.when(me > 0)
    def _():
        raw_up.wait_recv()

    @pl.when(me < n - 1)
    def _():
        raw_down.wait_recv()

    turn(planes + 1)
    turn(0)
    for line in range(height + 2):
        put_row(high, 1, planes + 1, line)

    def between(j):
        top = height + 2 if j == windows - 1 else 2 * j + 2
        put_rows(low, 1, range(2 * j, top))
        put_rows(x2, 0, range(2 * j, top))

    product(pairs - 1, low, high, between)

    cost_up = send(acc.at[planes + 1], prev, csem, 0, {"disp": up})
    cost_down = send(acc.at[0], following, csem, 1, {"disp": down})
    extra_up = send(exst.at[pairs - 1], exdiag.at[0], csem, 2, far)
    extra_down = send(exst.at[0], exdiag.at[1], csem, 3, near)
    extra(pairs - 1).start()

    @pl.when(me < n - 1)
    def _():
        cost_up.start()
        extra_up.start()

    product(0, x2, low, lambda j: None)
    extra(0).start()

    @pl.when(me > 0)
    def _():
        cost_down.start()
        extra_down.start()

    @pl.when(me < n - 1)
    def _():
        raw_up.wait_send()
        last_far.wait_send()

    @pl.when(me > 0)
    def _():
        raw_down.wait_send()
        first_near.wait_send()

    last_line.wait_send()
    first_line.wait_send()

    def line_sent(s, carry):
        lines(s).wait_send()
        return carry

    lax.fori_loop(1, pairs, line_sent, 0)

    mine = lax.broadcasted_iota(jnp.int32, (height, width), 0) == (1 - r) * (height - 1)

    def add_row(index, value):
        acc[index] += jnp.where(mine, jnp.broadcast_to(value, (height, width)), 0.0)

    def collect(k, carry):
        extra(k).wait()
        for q in range(4):
            add_row(2 * k + q, exin[k, q : q + 1, :])
        return carry

    def collect_end(k):
        extra(k).wait()
        for q in range(4):
            if 1 <= 2 * k + q <= planes:
                add_row(2 * k + q, exin[k, q : q + 1, :])

    lax.fori_loop(1, pairs - 1, collect, 0)
    collect_end(pairs - 1)
    collect_end(0)

    @pl.when(me > 0)
    def _():
        cost_up.wait_recv()
        extra_up.wait_recv()
        acc[1] += prev[...]
        add_row(1, exdiag[0, 3:4, :])

    @pl.when(me < n - 1)
    def _():
        cost_down.wait_recv()
        extra_down.wait_recv()
        acc[planes] += following[...]
        add_row(planes, exdiag[1, 0:1, :])

    low_cost = acc[1]
    for p in range(2, planes + 1):
        low_cost = jnp.minimum(low_cost, acc[p])
    base = (me * planes).astype(F32)
    total = jnp.zeros((height, width), F32)
    moment = jnp.zeros((height, width), F32)
    for p in range(planes):
        expo = jnp.exp(low_cost - acc[p + 1])
        total += expo
        moment += (base + float(p)) * expo
    peak = -low_cost

    @pl.when(me < n - 1)
    def _():
        cost_up.wait_send()
        extra_up.wait_send()

    @pl.when(me > 0)
    def _():
        cost_down.wait_send()
        extra_down.wait_send()

    if not whole:
        out[0] = peak
        out[1] = total
        out[2] = moment
        return

    def place(k):
        at = (k // across) * 8, (k % across) * LANES
        return slice(at[0], at[0] + 8), slice(at[1], at[1] + LANES)

    for k in range(n):
        rows, cols = place(k)
        stats[k, 0] = peak[rows, cols]
        stats[k, 1] = total[rows, cols]
        stats[k, 2] = moment[rows, cols]

    copies = []
    for j in range(1, n):
        peer = lax.rem(me + j, n)
        copies.append(send(stats.at[peer], taken.at[j], each, j, {"disp": peer}))
        copies[-1].start()
    for copy in copies:
        copy.wait()
    parts = [stats[me]] + [taken[j] for j in range(1, n)]
    top = parts[0][0]
    for part in parts[1:]:
        top = jnp.maximum(top, part[0])
    total = jnp.zeros_like(top)
    moment = jnp.zeros_like(top)
    for part in parts:
        scale = jnp.exp(part[0] - top)
        total += part[1] * scale
        moment += part[2] * scale
    final[me] = moment / total

    copies = []
    for j in range(1, n):
        peer = lax.rem(me + j, n)
        copies.append(send(final.at[me], final.at[me], each, n + j, {"disp": peer}))
        copies[-1].start()
    for copy in copies:
        copy.wait()
    for k in range(n):
        rows, cols = place(k)
        out[rows, cols] = final[k]


def body(volume, conv_weight, conv_bias, reg_weight):
    ch, planes, height, width = volume.shape
    n = lax.axis_size("disp")
    pairs = planes // 2
    whole = height * width == 8 * LANES * n
    lines = (height + 2) * ch
    slab = pltpu.VMEM((2, 3, lines, width), BF)
    vmem = pl.BlockSpec(memory_space=pltpu.VMEM)
    depth = 48 * ch
    flops = 2 * 4 * ch * depth * width * (height // 2) * pairs
    result = pl.pallas_call(
        functools.partial(main_kernel, whole),
        in_specs=[pl.BlockSpec(memory_space=pl.ANY), vmem, vmem, vmem],
        out_specs=vmem,
        out_shape=jax.ShapeDtypeStruct((height, width) if whole else (3, height, width), F32),
        scratch_shapes=[
            pltpu.VMEM((planes + 2, ch, height, width), BF),
            pltpu.VMEM((planes + 2, height, ch, width), BF),
            slab,
            slab,
            slab,
            pltpu.VMEM((2 * ch * height, width), BF),
            pltpu.VMEM((planes + 2, ch, width), BF),
            pltpu.VMEM((planes + 2, ch, width), BF),
            pltpu.VMEM((4 * ch, depth), BF),
            pltpu.VMEM((12 * height + 24, 2 * ch * height), BF),
            pltpu.VMEM((4 * ch, LANES), F32),
            pltpu.VMEM((planes + 2, height, width), F32),
            pltpu.VMEM((pairs, 8, width), F32),
            pltpu.VMEM((pairs, 8, width), F32),
            pltpu.VMEM((2, 8, width), F32),
            pltpu.VMEM((height, width), F32),
            pltpu.VMEM((height, width), F32),
            pltpu.VMEM((n, 3, 8, LANES), F32),
            pltpu.VMEM((n, 3, 8, LANES), F32),
            pltpu.VMEM((n, 8, LANES), F32),
            pltpu.SemaphoreType.DMA((planes,)),
            pltpu.SemaphoreType.DMA((2, 2)),
            pltpu.SemaphoreType.DMA((2, pairs + 3)),
            pltpu.SemaphoreType.DMA((2, pairs)),
            pltpu.SemaphoreType.DMA((2, 4)),
            pltpu.SemaphoreType.DMA((2, 2 * n)),
        ],
        compiler_params=pltpu.CompilerParams(collective_id=0, has_side_effects=True, vmem_limit_bytes=56 << 20),
        cost_estimate=pl.CostEstimate(flops=flops, bytes_accessed=2 * volume.size, transcendentals=0),
        name="fused",
    )(volume, conv_weight, conv_bias[:, None], reg_weight)
    if whole:
        return result
    value = joined(result, "disp")
    return value[2] / value[1]


def solution(mesh):
    in_specs = (P(None, "disp", ("tiles", "rows"), None), P(), P(), P())
    out_specs = P(("tiles", "rows"), None)
    return jax.shard_map(body, mesh=mesh, in_specs=in_specs, out_specs=out_specs, check_vma=False)
```

```python
import functools

import jax
import jax.numpy as jnp
from jax import lax
from jax.experimental import pallas as pl
from jax.experimental.pallas import tpu as pltpu
from jax.sharding import PartitionSpec as P

BF = jnp.bfloat16
F32 = jnp.float32
MESH = pl.DeviceIdType.MESH
LANES = 128


def combine(first, second):
    peak = jnp.maximum(first[0], second[0])
    left = jnp.exp(first[0] - peak)
    right = jnp.exp(second[0] - peak)
    return jnp.stack((peak, first[1] * left + second[1] * right, first[2] * left + second[2] * right))


def joined(value, axis):
    count = lax.axis_size(axis)
    if count & (count - 1):
        pieces = lax.all_gather(value, axis)
        running = pieces[0]
        for i in range(1, count):
            running = combine(running, pieces[i])
        return running
    step = 1
    while step < count:
        other = lax.ppermute(value, axis, [(i, i ^ step) for i in range(count)])
        value = combine(value, other)
        step *= 2
    return value


def moved(x, step):
    width = x.shape[1]
    rolled = pltpu.roll(x, step % width, 1)
    lane = lax.broadcasted_iota(jnp.int32, x.shape, 1)
    return jnp.where(lane == (0 if step == 1 else width - 1), jnp.zeros((), x.dtype), rolled)


def fill_a(cw, a_ref):
    ch = cw.shape[1]
    empty = jnp.zeros((ch, ch), F32)
    for a in range(3):
        for c in range(3):
            taps = [cw[9 * a + 3 * b + c].astype(F32) for b in range(3)]
            for r in range(2):
                parts = [taps[s - r] if 0 <= s - r < 3 else empty for s in range(4)]
                block = jnp.concatenate(parts, axis=1).astype(BF)
                for p in range(2):
                    col = ((a + p) * 3 + c) * 4 * ch
                    row = (2 * p + r) * ch
                    a_ref[row : row + ch, col : col + 4 * ch] = block
    zero = jnp.zeros((2 * ch, 12 * ch), BF)
    a_ref[: 2 * ch, 36 * ch :] = zero
    a_ref[2 * ch :, : 12 * ch] = zero


def fill_r(rw, r_ref, height, side):
    ch = rw.shape[1]
    span = 4 * ch
    lane = lax.broadcasted_iota(jnp.int32, (height, span), 1)
    odd = (lane // ch) % 2
    row = lax.broadcasted_iota(jnp.int32, (height, span), 0)
    lane8 = lax.broadcasted_iota(jnp.int32, (8, span), 1)
    odd8 = (lane8 // ch) % 2
    row8 = lax.broadcasted_iota(jnp.int32, (8, span), 0)
    empty = jnp.zeros((1, 2 * ch), F32)

    def line(q, c, b):
        parts = []
        for p in range(2):
            a = p - q + 2
            if 0 <= a < 3:
                t = 9 * a + 3 * b + c
                w = rw[t : t + 1, :].astype(F32)
                parts += [w, w]
            else:
                parts.append(empty)
        return jnp.concatenate(parts, axis=1)

    count = height // 2
    for c in range(3):
        edge_low = jnp.zeros((8, span), F32)
        edge_high = jnp.zeros((8, span), F32)
        for q in range(4):
            lines = [line(q, c, b) for b in range(3)]
            base = (3 * q + c) * height
            for j in range(count):
                place = 2 * j + odd + 1 - row
                out = jnp.zeros((height, span), F32)
                for b in range(3):
                    out = jnp.where(place == b, lines[b], out)
                r_ref[base : base + height, span * j : span * (j + 1)] = out.astype(BF)
            edge_low = jnp.where((row8 == q) & (odd8 == 0), lines[2], edge_low)
            edge_high = jnp.where((row8 == q) & (odd8 == 1), lines[0], edge_high)
        base = 12 * height + 8 * c
        low = jnp.where(side == 1, edge_low, 0.0)
        high = jnp.where(side == 0, edge_high, 0.0)
        for j in range(count):
            value = jnp.zeros((8, span), F32)
            if j == 0:
                value = value + low
            if j == count - 1:
                value = value + high
            r_ref[base : base + 8, span * j : span * (j + 1)] = value.astype(BF)


def main_kernel(
    whole, vol, cw, cb, rw, out, vbuf, tb, x0, x1, x2, hid, sline, hal, a_ref, r_ref, bias, acc, exst, exin, exdiag,
    prev, following, stats, taken, final, vsem, hsem, lsem, esem, csem, each,
):
    ch, planes, height, width = vol.shape
    pairs = planes // 2
    inner = pairs - 2
    windows = height // 2
    n = lax.axis_size("disp")
    me = lax.axis_index("disp")
    r = lax.axis_index("rows")
    up = jnp.minimum(me + 1, n - 1)
    down = jnp.maximum(me - 1, 0)
    xs = (x0, x1)

    def send(src, dst, sems, index, where):
        return pltpu.make_async_remote_copy(
            src_ref=src,
            dst_ref=dst,
            send_sem=sems.at[0, index],
            recv_sem=sems.at[1, index],
            device_id=where,
            device_id_type=MESH,
        )

    def load(p):
        return pltpu.make_async_copy(vol.at[:, p], vbuf.at[p + 1], vsem.at[p])

    load(planes - 1).start()
    load(0).start()

    def start_load(p, carry):
        load(p).start()
        return carry

    lax.fori_loop(1, planes - 1, start_load, 0)

    barrier = pltpu.get_barrier_semaphore()
    pl.semaphore_signal(barrier, inc=1, device_id={"rows": 1 - r}, device_id_type=MESH)
    for j in range(1, n):
        pl.semaphore_signal(barrier, inc=1, device_id={"disp": lax.rem(me + j, n)}, device_id_type=MESH)
    for j in (1, n - 1):
        where = {"disp": lax.rem(me + j, n), "rows": 1 - r}
        pl.semaphore_signal(barrier, inc=1, device_id=where, device_id_type=MESH)
    pl.semaphore_wait(barrier, n + 2)

    raw_up = send(vol.at[:, planes - 1], vbuf.at[0], hsem, 0, {"disp": up})
    raw_down = send(vol.at[:, 0], vbuf.at[planes + 1], hsem, 1, {"disp": down})

    piece = 4
    pieces = ch // piece

    def raw(t):
        rows = pl.ds(t * piece, piece)

        @pl.when(me < n - 1)
        def _():
            send(vol.at[rows, planes - 1], vbuf.at[0, rows], hsem, 0, {"disp": up}).start()

        @pl.when(me > 0)
        def _():
            send(vol.at[rows, 0], vbuf.at[planes + 1, rows], hsem, 1, {"disp": down}).start()

    raw(0)

    @pl.when(me == 0)
    def _():
        vbuf[0] = jnp.zeros((ch, height, width), BF)
        hal[0] = jnp.zeros((ch, width), BF)

    @pl.when(me == n - 1)
    def _():
        vbuf[planes + 1] = jnp.zeros((ch, height, width), BF)
        hal[planes + 1] = jnp.zeros((ch, width), BF)

    tb[2 * pairs + 1] = jnp.zeros((height, ch, width), BF)

    across = width // LANES
    edge = (height - 1) * (1 - r)

    def turn_part(index, part):
        cols = slice(part * LANES, (part + 1) * LANES)
        tb[index, :, :, cols] = jnp.swapaxes(vbuf[index, :, :, cols], 0, 1)

    def turn(index):
        for part in range(across):
            turn_part(index, part)

    far = {"disp": up, "rows": 1 - r}
    near = {"disp": down, "rows": 1 - r}
    last_line = send(sline.at[planes], hal.at[planes], lsem, pairs, {"rows": 1 - r})
    first_line = send(sline.at[1], hal.at[1], lsem, 0, {"rows": 1 - r})
    last_far = send(sline.at[planes], hal.at[0], lsem, pairs + 1, far)
    first_near = send(sline.at[1], hal.at[planes + 1], lsem, pairs + 2, near)

    def lines(s):
        both = pl.ds(2 * s, 2)
        return send(sline.at[both], hal.at[both], lsem, s, {"rows": 1 - r})

    def post(s):
        for f in range(2):
            sline[2 * s + f] = tb[2 * s + f, edge]
        lines(s).start()

    def await_pair(s):
        load(2 * s - 1).wait()
        load(2 * s).wait()

    def early(s, carry):
        await_pair(s)
        for f in range(2):
            turn(2 * s + f)
        post(s)
        return carry

    lead = min(4, pairs - 1)
    lax.fori_loop(1, min(2, lead) + 1, early, 0)
    raw(1)
    fill_a(cw, a_ref)
    fill_r(rw, r_ref, height, r)
    one = lax.broadcasted_iota(jnp.int32, (ch, ch), 0) == lax.broadcasted_iota(jnp.int32, (ch, ch), 1)
    column = jnp.sum(jnp.where(one, jnp.broadcast_to(cb[...], (ch, ch)), 0.0), axis=1, keepdims=True)
    bias[...] = jnp.concatenate([jnp.broadcast_to(column, (ch, LANES))] * 4, axis=0)
    acc[...] = jnp.zeros_like(acc)
    lax.fori_loop(min(2, lead) + 1, lead + 1, early, 0)
    load(planes - 1).wait()
    load(0).wait()
    for index in (planes, 1):
        turn(index)
        sline[index] = tb[index, edge]
    last_line.start()
    first_line.start()

    @pl.when(me < n - 1)
    def _():
        last_far.start()

    @pl.when(me > 0)
    def _():
        first_near.start()


    def put_row(x, f, index, line):
        if line == 0:
            value = hal[index]
            value = jnp.where(r == 1, value, jnp.zeros_like(value))
        elif line == height + 1:
            value = hal[index]
            value = jnp.where(r == 0, value, jnp.zeros_like(value))
        else:
            value = tb[index, line - 1]
        at = slice(line * ch, (line + 1) * ch)
        x[f, 0, at, :] = moved(value, 1)
        x[f, 1, at, :] = value
        x[f, 2, at, :] = moved(value, -1)

    def put_rows(x, s, lines_):
        for line in lines_:
            for f in range(2):
                put_row(x, f, 2 * s + f, line)

    def product(k, low, high, between):
        for j in range(windows):
            rows = slice(2 * j * ch, (2 * j + 4) * ch)
            x = jnp.concatenate([x[f, c, rows, :] for x in (low, high) for f in range(2) for c in range(3)], axis=0)
            pre = jnp.dot(a_ref[...], x, preferred_element_type=F32) + jnp.tile(bias[...], (1, across))
            hid[4 * ch * j : 4 * ch * (j + 1), :] = jnp.maximum(pre, 0.0).astype(BF)
            between(j)
        part = jnp.dot(r_ref[...], hid[...], preferred_element_type=F32)

        def gathered(base, step, size):
            one, two, three = (part[base + step * c : base + step * c + size] for c in range(3))
            return moved(one, 1) + two + moved(three, -1)

        for q in range(4):
            acc[2 * k + q] += gathered(3 * q * height, height, height)
        exst[k] = gathered(12 * height, 8, 8)

    def extra(k):
        return send(exst.at[k], exin.at[k], esem, k, {"rows": 1 - r})

    for s in range(1, min(2, pairs - 1) + 1):
        put_rows(xs[s - 1], s, range(1, height + 1))
    raw(2)
    for s in range(1, min(2, pairs - 1) + 1):
        lines(s).wait_recv()
        put_rows(xs[s - 1], s, (0, height + 1))

    def step(i, parity):
        low, high = xs[parity], xs[1 - parity]
        ahead = jnp.minimum(i + lead + 1, pairs - 1)

        @pl.when(i + lead + 1 < pairs)
        def _():
            await_pair(ahead)

        @pl.when(i + 3 < pairs)
        def _():
            lines(i + 3).wait_recv()

        @pl.when(i == inner - 1)
        def _():
            last_line.wait_recv()
            first_line.wait_recv()

            @pl.when(me > 0)
            def _():
                last_far.wait_recv()

            @pl.when(me < n - 1)
            def _():
                first_near.wait_recv()

        parts = [(f, part) for f in range(2) for part in range(across)]

        def between(j):
            top = height + 2 if j == windows - 1 else 2 * j + 2
            put_rows(low, i + 3, range(2 * j, top))
            for f, part in parts[j * len(parts) // windows : (j + 1) * len(parts) // windows]:
                turn_part(2 * ahead + f, part)

        product(i + 1, low, high, between)

        @pl.when(i + lead + 1 < pairs)
        def _():
            post(ahead)

        @pl.when(i + 3 < pieces)
        def _():
            raw(i + 3)

        extra(i + 1).start()

    def two(t, carry):
        step(2 * t, 0)
        step(2 * t + 1, 1)
        return carry

    lax.fori_loop(0, inner // 2, two, 0)
    if inner % 2:
        step(inner - 1, 0)
    for t in range(inner + 3, pieces):
        raw(t)
    high, low = xs[(inner + 1) % 2], xs[inner % 2]

    @pl.when(me > 0)
    def _():
        raw_up.wait_recv()

    @pl.when(me < n - 1)
    def _():
        raw_down.wait_recv()

    turn(planes + 1)
    turn(0)
    for line in range(height + 2):
        put_row(high, 1, planes + 1, line)

    def between(j):
        top = height + 2 if j == windows - 1 else 2 * j + 2
        put_rows(low, 1, range(2 * j, top))
        put_rows(x2, 0, range(2 * j, top))

    product(pairs - 1, low, high, between)

    cost_up = send(acc.at[planes + 1], prev, csem, 0, {"disp": up})
    cost_down = send(acc.at[0], following, csem, 1, {"disp": down})
    extra_up = send(exst.at[pairs - 1], exdiag.at[0], csem, 2, far)
    extra_down = send(exst.at[0], exdiag.at[1], csem, 3, near)
    extra(pairs - 1).start()

    @pl.when(me < n - 1)
    def _():
        cost_up.start()
        extra_up.start()

    product(0, x2, low, lambda j: None)
    extra(0).start()

    @pl.when(me > 0)
    def _():
        cost_down.start()
        extra_down.start()

    @pl.when(me < n - 1)
    def _():
        raw_up.wait_send()
        last_far.wait_send()

    @pl.when(me > 0)
    def _():
        raw_down.wait_send()
        first_near.wait_send()

    last_line.wait_send()
    first_line.wait_send()

    def line_sent(s, carry):
        lines(s).wait_send()
        return carry

    lax.fori_loop(1, pairs, line_sent, 0)

    mine = lax.broadcasted_iota(jnp.int32, (height, width), 0) == (1 - r) * (height - 1)

    def add_row(index, value):
        acc[index] += jnp.where(mine, jnp.broadcast_to(value, (height, width)), 0.0)

    def collect(k, carry):
        extra(k).wait()
        for q in range(4):
            add_row(2 * k + q, exin[k, q : q + 1, :])
        return carry

    def collect_end(k):
        extra(k).wait()
        for q in range(4):
            if 1 <= 2 * k + q <= planes:
                add_row(2 * k + q, exin[k, q : q + 1, :])

    lax.fori_loop(1, pairs - 1, collect, 0)
    collect_end(pairs - 1)
    collect_end(0)

    @pl.when(me > 0)
    def _():
        cost_up.wait_recv()
        extra_up.wait_recv()
        acc[1] += prev[...]
        add_row(1, exdiag[0, 3:4, :])

    @pl.when(me < n - 1)
    def _():
        cost_down.wait_recv()
        extra_down.wait_recv()
        acc[planes] += following[...]
        add_row(planes, exdiag[1, 0:1, :])

    low_cost = acc[1]
    for p in range(2, planes + 1):
        low_cost = jnp.minimum(low_cost, acc[p])
    base = (me * planes).astype(F32)
    total = jnp.zeros((height, width), F32)
    moment = jnp.zeros((height, width), F32)
    for p in range(planes):
        expo = jnp.exp(low_cost - acc[p + 1])
        total += expo
        moment += (base + float(p)) * expo
    peak = -low_cost

    @pl.when(me < n - 1)
    def _():
        cost_up.wait_send()
        extra_up.wait_send()

    @pl.when(me > 0)
    def _():
        cost_down.wait_send()
        extra_down.wait_send()

    if not whole:
        out[0] = peak
        out[1] = total
        out[2] = moment
        return

    def place(k):
        at = (k // across) * 8, (k % across) * LANES
        return slice(at[0], at[0] + 8), slice(at[1], at[1] + LANES)

    for k in range(n):
        rows, cols = place(k)
        stats[k, 0] = peak[rows, cols]
        stats[k, 1] = total[rows, cols]
        stats[k, 2] = moment[rows, cols]

    copies = []
    for j in range(1, n):
        peer = lax.rem(me + j, n)
        copies.append(send(stats.at[peer], taken.at[j], each, j, {"disp": peer}))
        copies[-1].start()
    for copy in copies:
        copy.wait()
    parts = [stats[me]] + [taken[j] for j in range(1, n)]
    top = parts[0][0]
    for part in parts[1:]:
        top = jnp.maximum(top, part[0])
    total = jnp.zeros_like(top)
    moment = jnp.zeros_like(top)
    for part in parts:
        scale = jnp.exp(part[0] - top)
        total += part[1] * scale
        moment += part[2] * scale
    final[me] = moment / total

    copies = []
    for j in range(1, n):
        peer = lax.rem(me + j, n)
        copies.append(send(final.at[me], final.at[me], each, n + j, {"disp": peer}))
        copies[-1].start()
    for copy in copies:
        copy.wait()
    for k in range(n):
        rows, cols = place(k)
        out[rows, cols] = final[k]


def body(volume, conv_weight, conv_bias, reg_weight):
    ch, planes, height, width = volume.shape
    n = lax.axis_size("disp")
    pairs = planes // 2
    whole = height * width == 8 * LANES * n
    lines = (height + 2) * ch
    slab = pltpu.VMEM((2, 3, lines, width), BF)
    vmem = pl.BlockSpec(memory_space=pltpu.VMEM)
    depth = 48 * ch
    flops = 2 * 4 * ch * depth * width * (height // 2) * pairs
    result = pl.pallas_call(
        functools.partial(main_kernel, whole),
        in_specs=[pl.BlockSpec(memory_space=pl.ANY), vmem, vmem, vmem],
        out_specs=vmem,
        out_shape=jax.ShapeDtypeStruct((height, width) if whole else (3, height, width), F32),
        scratch_shapes=[
            pltpu.VMEM((planes + 2, ch, height, width), BF),
            pltpu.VMEM((planes + 2, height, ch, width), BF),
            slab,
            slab,
            slab,
            pltpu.VMEM((2 * ch * height, width), BF),
            pltpu.VMEM((planes + 2, ch, width), BF),
            pltpu.VMEM((planes + 2, ch, width), BF),
            pltpu.VMEM((4 * ch, depth), BF),
            pltpu.VMEM((12 * height + 24, 2 * ch * height), BF),
            pltpu.VMEM((4 * ch, LANES), F32),
            pltpu.VMEM((planes + 2, height, width), F32),
            pltpu.VMEM((pairs, 8, width), F32),
            pltpu.VMEM((pairs, 8, width), F32),
            pltpu.VMEM((2, 8, width), F32),
            pltpu.VMEM((height, width), F32),
            pltpu.VMEM((height, width), F32),
            pltpu.VMEM((n, 3, 8, LANES), F32),
            pltpu.VMEM((n, 3, 8, LANES), F32),
            pltpu.VMEM((n, 8, LANES), F32),
            pltpu.SemaphoreType.DMA((planes,)),
            pltpu.SemaphoreType.DMA((2, 2)),
            pltpu.SemaphoreType.DMA((2, pairs + 3)),
            pltpu.SemaphoreType.DMA((2, pairs)),
            pltpu.SemaphoreType.DMA((2, 4)),
            pltpu.SemaphoreType.DMA((2, 2 * n)),
        ],
        compiler_params=pltpu.CompilerParams(collective_id=0, has_side_effects=True, vmem_limit_bytes=56 << 20),
        cost_estimate=pl.CostEstimate(flops=flops, bytes_accessed=2 * volume.size, transcendentals=0),
        name="fused",
    )(volume, conv_weight, conv_bias[None, :], reg_weight)
    if whole:
        return result
    value = joined(result, "disp")
    return value[2] / value[1]


def solution(mesh):
    in_specs = (P(None, "disp", ("tiles", "rows"), None), P(), P(), P())
    out_specs = P(("tiles", "rows"), None)
    return jax.shard_map(body, mesh=mesh, in_specs=in_specs, out_specs=out_specs, check_vma=False)
```

```python
import functools

import jax
import jax.numpy as jnp
from jax import lax
from jax.experimental import pallas as pl
from jax.experimental.pallas import tpu as pltpu
from jax.sharding import PartitionSpec as P

BF = jnp.bfloat16
F32 = jnp.float32
MESH = pl.DeviceIdType.MESH
LANES = 128


def combine(first, second):
    peak = jnp.maximum(first[0], second[0])
    left = jnp.exp(first[0] - peak)
    right = jnp.exp(second[0] - peak)
    return jnp.stack((peak, first[1] * left + second[1] * right, first[2] * left + second[2] * right))


def joined(value, axis):
    count = lax.axis_size(axis)
    if count & (count - 1):
        pieces = lax.all_gather(value, axis)
        running = pieces[0]
        for i in range(1, count):
            running = combine(running, pieces[i])
        return running
    step = 1
    while step < count:
        other = lax.ppermute(value, axis, [(i, i ^ step) for i in range(count)])
        value = combine(value, other)
        step *= 2
    return value


def moved(x, step):
    width = x.shape[1]
    rolled = pltpu.roll(x, step % width, 1)
    lane = lax.broadcasted_iota(jnp.int32, x.shape, 1)
    return jnp.where(lane == (0 if step == 1 else width - 1), jnp.zeros((), x.dtype), rolled)


def fill_a(cw, a_ref):
    ch = cw.shape[1]
    empty = jnp.zeros((ch, ch), F32)
    for a in range(3):
        for c in range(3):
            taps = [cw[9 * a + 3 * b + c].astype(F32) for b in range(3)]
            for r in range(2):
                parts = [taps[s - r] if 0 <= s - r < 3 else empty for s in range(4)]
                block = jnp.concatenate(parts, axis=1).astype(BF)
                for p in range(2):
                    col = ((a + p) * 3 + c) * 4 * ch
                    row = (2 * p + r) * ch
                    a_ref[row : row + ch, col : col + 4 * ch] = block
    zero = jnp.zeros((2 * ch, 12 * ch), BF)
    a_ref[: 2 * ch, 36 * ch :] = zero
    a_ref[2 * ch :, : 12 * ch] = zero


def fill_r(rw, r_ref):
    ch = rw.shape[1]
    span = 4 * ch
    row = lax.broadcasted_iota(jnp.int32, (8, span), 0)
    odd = (lax.broadcasted_iota(jnp.int32, (8, span), 1) // ch) % 2
    empty = jnp.zeros((1, 2 * ch), F32)

    def line(q, c, b):
        parts = []
        for p in range(2):
            a = p - q + 2
            if 0 <= a < 3:
                t = 9 * a + 3 * b + c
                w = rw[t : t + 1, :].astype(F32)
                parts += [w, w]
            else:
                parts.append(empty)
        return jnp.concatenate(parts, axis=1)

    blocks = []
    edges = []
    for c in range(3):
        above = jnp.zeros((8, span), F32)
        below = jnp.zeros((8, span), F32)
        for q in range(4):
            lines = [line(q, c, b) for b in range(3)]
            above = jnp.where((row == q) & (odd == 0), lines[2], above)
            below = jnp.where((row == 4 + q) & (odd == 1), lines[0], below)
            parts = []
            for j in range(4):
                place = 2 * j + odd + 1 - row
                out = jnp.zeros((8, span), F32)
                for b in range(3):
                    out = jnp.where(place == b, lines[b], out)
                parts.append(out)
            blocks.append((q, c, jnp.concatenate(parts, axis=1)))
        zero = jnp.zeros((8, span), F32)
        edges.append(jnp.concatenate([above, zero, zero, below], axis=1))
    blocks.sort(key=lambda item: item[:2])
    rows = [block for _, _, block in blocks] + edges + [jnp.zeros((8, 4 * span), F32)]
    r_ref[...] = jnp.concatenate(rows, axis=0).astype(BF)


def main_kernel(
    whole, vol, cw, cb, rw, out, vbuf, tb, x0, x1, h0, h1, sline, hal, a_ref, r_ref, bias, acc, exst, exin, exdiag,
    prev, following, stats, taken, final, vsem, hsem, lsem, esem, csem, each,
):
    ch, planes, height, width = vol.shape
    pairs = planes // 2
    first = 1
    gap = pairs - first
    count = pairs + 1
    spare = pairs + 1
    windows = height // 2
    groups = height // 8
    n = lax.axis_size("disp")
    me = lax.axis_index("disp")
    r = lax.axis_index("rows")
    up = jnp.minimum(me + 1, n - 1)
    down = jnp.maximum(me - 1, 0)
    xs = (x0, x1)
    hids = (h0, h1)

    def pair_of(item):
        return jnp.where(item <= gap, first + item, item - gap - 1) if not isinstance(item, int) else (
            first + item if item <= gap else item - gap - 1
        )

    def turned(t):
        return (first + t if t < gap else t - gap + 1) if isinstance(t, int) else jnp.where(t < gap, first + t, t - gap + 1)

    def send(src, dst, sems, index, where):
        return pltpu.make_async_remote_copy(
            src_ref=src,
            dst_ref=dst,
            send_sem=sems.at[0, index],
            recv_sem=sems.at[1, index],
            device_id=where,
            device_id_type=MESH,
        )

    def load(p):
        return pltpu.make_async_copy(vol.at[:, p], vbuf.at[p + 1], vsem.at[p])

    def start_pair(t, carry):
        load(2 * turned(t) - 1).start()
        load(2 * turned(t)).start()
        return carry

    lead = min(2, pairs - 1)
    lax.fori_loop(0, lead, start_pair, 0)
    load(planes - 1).start()
    load(0).start()
    fetch = 3
    lax.fori_loop(lead, min(fetch, pairs - 1), start_pair, 0)

    barrier = pltpu.get_barrier_semaphore()
    pl.semaphore_signal(barrier, inc=1, device_id={"rows": 1 - r}, device_id_type=MESH)
    for j in range(1, n):
        pl.semaphore_signal(barrier, inc=1, device_id={"disp": lax.rem(me + j, n)}, device_id_type=MESH)
    for j in (1, n - 1):
        where = {"disp": lax.rem(me + j, n), "rows": 1 - r}
        pl.semaphore_signal(barrier, inc=1, device_id=where, device_id_type=MESH)
    piece = 4
    pieces = ch // piece

    def raw(t):
        rows = pl.ds(t * piece, piece)

        @pl.when(me < n - 1)
        def _():
            send(vol.at[rows, planes - 1], vbuf.at[0, rows], hsem, 0, {"disp": up}).start()

        @pl.when(me > 0)
        def _():
            send(vol.at[rows, 0], vbuf.at[planes + 1, rows], hsem, 1, {"disp": down}).start()


    @pl.when(me == 0)
    def _():
        vbuf[0] = jnp.zeros((ch, height, width), BF)
        hal[0] = jnp.zeros((ch, width), BF)

    @pl.when(me == n - 1)
    def _():
        vbuf[planes + 1] = jnp.zeros((ch, height, width), BF)
        hal[planes + 1] = jnp.zeros((ch, width), BF)

    across = width // LANES
    edge = (height - 1) * (1 - r)

    def turn_part(index, part):
        cols = slice(part * LANES, (part + 1) * LANES)
        tb[index, :, :, cols] = jnp.swapaxes(vbuf[index, :, :, cols], 0, 1)

    def turn(index):
        for part in range(across):
            turn_part(index, part)

    far = {"disp": up, "rows": 1 - r}
    near = {"disp": down, "rows": 1 - r}
    last_line = send(sline.at[planes], hal.at[planes], lsem, pairs, {"rows": 1 - r})
    first_line = send(sline.at[1], hal.at[1], lsem, 0, {"rows": 1 - r})
    last_far = send(sline.at[planes], hal.at[0], lsem, pairs + 1, far)
    first_near = send(sline.at[1], hal.at[planes + 1], lsem, pairs + 2, near)

    def lines(s):
        both = pl.ds(2 * s, 2)
        return send(sline.at[both], hal.at[both], lsem, s, {"rows": 1 - r})

    def keep(t):
        s = turned(t)
        await_pair(s)

        @pl.when(t + fetch < pairs - 1)
        def _():
            start_pair(t + fetch, 0)

        for f in range(2):
            turn(2 * s + f)
            sline[2 * s + f] = tb[2 * s + f, edge]

    def await_pair(s):
        load(2 * s - 1).wait()
        load(2 * s).wait()

    def early(t, carry):
        keep(t)
        return carry

    def late(t, carry):
        keep(t)
        lines(turned(t)).start()

        @pl.when(t % 4 == 1)
        def _():
            raw((t - 1) // 4)

        return carry

    lax.fori_loop(0, lead, early, 0)
    pl.semaphore_wait(barrier, n + 2)

    raw_up = send(vol.at[:, planes - 1], vbuf.at[0], hsem, 0, {"disp": up})
    raw_down = send(vol.at[:, 0], vbuf.at[planes + 1], hsem, 1, {"disp": down})

    for t in range(lead):
        lines(turned(t)).start()
    raw(0)
    fill_a(cw, a_ref)
    fill_r(rw, r_ref)
    one = lax.broadcasted_iota(jnp.int32, (ch, ch), 0) == lax.broadcasted_iota(jnp.int32, (ch, ch), 1)
    column = jnp.sum(jnp.where(one, jnp.broadcast_to(cb[...], (ch, ch)), 0.0), axis=1, keepdims=True)
    bias[...] = jnp.concatenate([jnp.broadcast_to(column, (ch, LANES))] * 4, axis=0)
    acc[...] = jnp.zeros_like(acc)
    h1[...] = jnp.zeros_like(h1)
    load(planes - 1).wait()
    load(0).wait()
    for index in (planes, 1):
        turn(index)
        sline[index] = tb[index, edge]
    last_line.start()
    first_line.start()

    @pl.when(me < n - 1)
    def _():
        last_far.start()

    @pl.when(me > 0)
    def _():
        first_near.start()

    lax.fori_loop(lead, pairs - 1, late, 0)
    for t in range(1 + sum(t % 4 == 1 for t in range(lead, pairs - 1)), pieces):
        raw(t)

    def put_row(x, f, index, line):
        if line == 0:
            value = hal[index]
            value = jnp.where(r == 1, value, jnp.zeros_like(value))
        elif line == height + 1:
            value = hal[index]
            value = jnp.where(r == 0, value, jnp.zeros_like(value))
        else:
            value = tb[index, line - 1]
        at = slice(line * ch, (line + 1) * ch)
        x[f, 0, at, :] = moved(value, 1)
        x[f, 1, at, :] = value
        x[f, 2, at, :] = moved(value, -1)

    def put_rows(x, s, lines_):
        for line in lines_:
            for f in range(2):
                put_row(x, f, 2 * s + f, line)

    def regress(k, hid):
        for g in range(groups):
            span = 16 * ch
            part = jnp.dot(r_ref[...], hid[span * g : span * (g + 1), :], preferred_element_type=F32)

            def gathered(base, step):
                one, two, three = (part[base + step * c : base + step * c + 8] for c in range(3))
                return moved(one, 1) + two + moved(three, -1)

            rows = slice(8 * g, 8 * g + 8)
            for q in range(4):
                acc[2 * k + q, rows, :] += gathered(24 * q, 8)
            beyond = gathered(96, 8)
            if g > 0:
                for q in range(4):
                    acc[2 * k + q, 8 * g - 1 : 8 * g, :] += beyond[q : q + 1]
            if g < groups - 1:
                for q in range(4):
                    acc[2 * k + q, 8 * g + 8 : 8 * g + 9, :] += beyond[4 + q : 5 + q]
            if g == 0:
                exst[k, 0:4, :] = beyond[0:4]
            if g == groups - 1:
                exst[k, 4:8, :] = beyond[4:8]

    def product(low, high, hid, between):
        for j in range(windows):
            rows = slice(2 * j * ch, (2 * j + 4) * ch)
            x = jnp.concatenate([x[f, c, rows, :] for x in (low, high) for f in range(2) for c in range(3)], axis=0)
            pre = jnp.dot(a_ref[...], x, preferred_element_type=F32) + jnp.tile(bias[...], (1, across))
            hid[4 * ch * j : 4 * ch * (j + 1), :] = jnp.maximum(pre, 0.0).astype(BF)
            between(j)

    def extra(k):
        return send(exst.at[k], exin.at[k], esem, k, {"rows": 1 - r})

    cost_up = send(acc.at[planes + 1], prev, csem, 0, {"disp": up})
    cost_down = send(acc.at[0], following, csem, 1, {"disp": down})
    extra_up = send(exst.at[pairs - 1], exdiag.at[0], csem, 2, far)
    extra_down = send(exst.at[0], exdiag.at[1], csem, 3, near)

    def take_after():
        last_line.wait_recv()

        @pl.when(me < n - 1)
        def _():
            first_near.wait_recv()
            raw_down.wait_recv()

        turn(planes + 1)

    def take_before():
        first_line.wait_recv()

        @pl.when(me > 0)
        def _():
            last_far.wait_recv()
            raw_up.wait_recv()

        turn(0)

    for item in range(2):
        if item < gap:
            put_rows(xs[item], pair_of(item), range(1, height + 1))
    for item in range(2):
        if item < gap:
            lines(pair_of(item)).wait_recv()
            put_rows(xs[item], pair_of(item), (0, height + 1))
        else:
            take_after()
            put_rows(xs[item], pair_of(item), range(height + 2))

    def step(i, parity):
        low, high = xs[parity], xs[1 - parity]
        s = pair_of(i + 2)
        s = jnp.where(s > pairs, pairs, s)
        k = jnp.where((i == 0) | (i == gap + 1), spare, pair_of(i - 1))

        @pl.when((s > 0) & (s < pairs) & (i + 2 < count))
        def _():
            lines(s).wait_recv()

        @pl.when(i + 2 == gap)
        def _():
            take_after()

        @pl.when(i + 1 == gap)
        def _():
            take_before()

        def build(j):
            top = height + 2 if j == windows - 1 else 2 * j + 2
            put_rows(low, s, range(2 * j, top))

        def full():
            regress(k, hids[1 - parity])
            product(low, high, hids[parity], build)

        if parity != gap % 2:
            full()
        else:

            @pl.when(i != gap)
            def _():
                full()

            @pl.when(i == gap)
            def _():
                regress(k, hids[1 - parity])
                for j in range(windows):
                    build(j)

        @pl.when(k < pairs)
        def _():
            extra(k).start()

        @pl.when((i == gap) & (me < n - 1))
        def _():
            cost_up.start()
            extra_up.start()

    def two(t, carry):
        step(2 * t, 0)

        @pl.when(2 * t + 1 < count)
        def _():
            step(2 * t + 1, 1)

        return carry

    lax.fori_loop(0, (count + 1) // 2, two, 0)
    regress(first - 1, hids[(count - 1) % 2])
    extra(first - 1).start()

    @pl.when(me > 0)
    def _():
        cost_down.start()
        extra_down.start()

    @pl.when(me < n - 1)
    def _():
        raw_up.wait_send()
        last_far.wait_send()

    @pl.when(me > 0)
    def _():
        raw_down.wait_send()
        first_near.wait_send()

    last_line.wait_send()
    first_line.wait_send()

    def line_sent(s, carry):
        lines(s).wait_send()
        return carry

    lax.fori_loop(1, pairs, line_sent, 0)

    mine = lax.broadcasted_iota(jnp.int32, (height, width), 0) == (1 - r) * (height - 1)

    def add_row(index, value):
        acc[index] += jnp.where(mine, jnp.broadcast_to(value, (height, width)), 0.0)

    def collect(k, carry):
        extra(k).wait()
        for q in range(4):
            add_row(2 * k + q, exin[k, pl.ds(4 * r + q, 1), :])
        return carry

    def collect_end(k):
        extra(k).wait()
        for q in range(4):
            if 1 <= 2 * k + q <= planes:
                add_row(2 * k + q, exin[k, pl.ds(4 * r + q, 1), :])

    lax.fori_loop(first, pairs - 1, collect, 0)
    collect_end(pairs - 1)
    collect_end(0)

    @pl.when(me > 0)
    def _():
        cost_up.wait_recv()
        extra_up.wait_recv()
        acc[1] += prev[...]
        add_row(1, exdiag[0, pl.ds(4 * r + 3, 1), :])

    @pl.when(me < n - 1)
    def _():
        cost_down.wait_recv()
        extra_down.wait_recv()
        acc[planes] += following[...]
        add_row(planes, exdiag[1, pl.ds(4 * r, 1), :])

    for k in range(1, first):
        collect(k, 0)

    low_cost = acc[1]
    for p in range(2, planes + 1):
        low_cost = jnp.minimum(low_cost, acc[p])
    base = (me * planes).astype(F32)
    total = jnp.zeros((height, width), F32)
    moment = jnp.zeros((height, width), F32)
    for p in range(planes):
        expo = jnp.exp(low_cost - acc[p + 1])
        total += expo
        moment += (base + float(p)) * expo
    peak = -low_cost

    @pl.when(me < n - 1)
    def _():
        cost_up.wait_send()
        extra_up.wait_send()

    @pl.when(me > 0)
    def _():
        cost_down.wait_send()
        extra_down.wait_send()

    if not whole:
        out[0] = peak
        out[1] = total
        out[2] = moment
        return

    def place(k):
        at = (k // across) * 8, (k % across) * LANES
        return slice(at[0], at[0] + 8), slice(at[1], at[1] + LANES)

    for k in range(n):
        rows, cols = place(k)
        stats[k, 0] = peak[rows, cols]
        stats[k, 1] = total[rows, cols]
        stats[k, 2] = moment[rows, cols]

    copies = []
    for j in range(1, n):
        peer = lax.rem(me + j, n)
        copies.append(send(stats.at[peer], taken.at[j], each, j, {"disp": peer}))
        copies[-1].start()
    for copy in copies:
        copy.wait()
    parts = [stats[me]] + [taken[j] for j in range(1, n)]
    top = parts[0][0]
    for part in parts[1:]:
        top = jnp.maximum(top, part[0])
    total = jnp.zeros_like(top)
    moment = jnp.zeros_like(top)
    for part in parts:
        scale = jnp.exp(part[0] - top)
        total += part[1] * scale
        moment += part[2] * scale
    final[me] = moment / total

    copies = []
    for j in range(1, n):
        peer = lax.rem(me + j, n)
        copies.append(send(final.at[me], final.at[me], each, n + j, {"disp": peer}))
        copies[-1].start()
    for copy in copies:
        copy.wait()
    for k in range(n):
        rows, cols = place(k)
        out[rows, cols] = final[k]


def body(volume, conv_weight, conv_bias, reg_weight):
    ch, planes, height, width = volume.shape
    n = lax.axis_size("disp")
    pairs = planes // 2
    whole = height * width == 8 * LANES * n
    lines = (height + 2) * ch
    slab = pltpu.VMEM((2, 3, lines, width), BF)
    vmem = pl.BlockSpec(memory_space=pltpu.VMEM)
    depth = 48 * ch
    flops = 2 * 4 * ch * depth * width * (height // 2) * pairs
    result = pl.pallas_call(
        functools.partial(main_kernel, whole),
        in_specs=[pl.BlockSpec(memory_space=pl.ANY), vmem, vmem, vmem],
        out_specs=vmem,
        out_shape=jax.ShapeDtypeStruct((height, width) if whole else (3, height, width), F32),
        scratch_shapes=[
            pltpu.VMEM((planes + 2, ch, height, width), BF),
            pltpu.VMEM((planes + 2, height, ch, width), BF),
            slab,
            slab,
            pltpu.VMEM((2 * ch * height, width), BF),
            pltpu.VMEM((2 * ch * height, width), BF),
            pltpu.VMEM((planes + 2, ch, width), BF),
            pltpu.VMEM((planes + 2, ch, width), BF),
            pltpu.VMEM((4 * ch, depth), BF),
            pltpu.VMEM((128, 16 * ch), BF),
            pltpu.VMEM((4 * ch, LANES), F32),
            pltpu.VMEM((planes + 6, height, width), F32),
            pltpu.VMEM((pairs + 2, 8, width), F32),
            pltpu.VMEM((pairs, 8, width), F32),
            pltpu.VMEM((2, 8, width), F32),
            pltpu.VMEM((height, width), F32),
            pltpu.VMEM((height, width), F32),
            pltpu.VMEM((n, 3, 8, LANES), F32),
            pltpu.VMEM((n, 3, 8, LANES), F32),
            pltpu.VMEM((n, 8, LANES), F32),
            pltpu.SemaphoreType.DMA((planes,)),
            pltpu.SemaphoreType.DMA((2, 2)),
            pltpu.SemaphoreType.DMA((2, pairs + 3)),
            pltpu.SemaphoreType.DMA((2, pairs)),
            pltpu.SemaphoreType.DMA((2, 4)),
            pltpu.SemaphoreType.DMA((2, 2 * n)),
        ],
        compiler_params=pltpu.CompilerParams(collective_id=0, has_side_effects=True, vmem_limit_bytes=56 << 20),
        cost_estimate=pl.CostEstimate(flops=flops, bytes_accessed=2 * volume.size, transcendentals=0),
        name="fused",
    )(volume, conv_weight, conv_bias[None, :], reg_weight)
    if whole:
        return result
    value = joined(result, "disp")
    return value[2] / value[1]


def solution(mesh):
    in_specs = (P(None, "disp", ("tiles", "rows"), None), P(), P(), P())
    out_specs = P(("tiles", "rows"), None)
    return jax.shard_map(body, mesh=mesh, in_specs=in_specs, out_specs=out_specs, check_vma=False)
```

```python
import functools

import jax
import jax.numpy as jnp
from jax import lax
from jax.experimental import pallas as pl
from jax.experimental.pallas import tpu as pltpu
from jax.sharding import PartitionSpec as P

BF = jnp.bfloat16
F32 = jnp.float32
MESH = pl.DeviceIdType.MESH
LANES = 128


def combine(first, second):
    peak = jnp.maximum(first[0], second[0])
    left = jnp.exp(first[0] - peak)
    right = jnp.exp(second[0] - peak)
    return jnp.stack((peak, first[1] * left + second[1] * right, first[2] * left + second[2] * right))


def joined(value, axis):
    count = lax.axis_size(axis)
    if count & (count - 1):
        pieces = lax.all_gather(value, axis)
        running = pieces[0]
        for i in range(1, count):
            running = combine(running, pieces[i])
        return running
    step = 1
    while step < count:
        other = lax.ppermute(value, axis, [(i, i ^ step) for i in range(count)])
        value = combine(value, other)
        step *= 2
    return value


def moved(x, step):
    width = x.shape[1]
    rolled = pltpu.roll(x, step % width, 1)
    lane = lax.broadcasted_iota(jnp.int32, x.shape, 1)
    return jnp.where(lane == (0 if step == 1 else width - 1), jnp.zeros((), x.dtype), rolled)


def fill_a(cw, a_ref):
    ch = cw.shape[1]
    empty = jnp.zeros((ch, ch), F32)
    for a in range(3):
        for c in range(3):
            taps = [cw[9 * a + 3 * b + c].astype(F32) for b in range(3)]
            for r in range(2):
                parts = [taps[s - r] if 0 <= s - r < 3 else empty for s in range(4)]
                block = jnp.concatenate(parts, axis=1).astype(BF)
                for p in range(2):
                    col = ((a + p) * 3 + c) * 4 * ch
                    row = (2 * p + r) * ch
                    a_ref[row : row + ch, col : col + 4 * ch] = block
    zero = jnp.zeros((2 * ch, 12 * ch), BF)
    a_ref[: 2 * ch, 36 * ch :] = zero
    a_ref[2 * ch :, : 12 * ch] = zero


def fill_r(rw, r_ref):
    ch = rw.shape[1]
    span = 4 * ch
    row = lax.broadcasted_iota(jnp.int32, (8, span), 0)
    odd = (lax.broadcasted_iota(jnp.int32, (8, span), 1) // ch) % 2
    empty = jnp.zeros((1, 2 * ch), F32)

    def line(q, c, b):
        parts = []
        for p in range(2):
            a = p - q + 2
            if 0 <= a < 3:
                t = 9 * a + 3 * b + c
                w = rw[t : t + 1, :].astype(F32)
                parts += [w, w]
            else:
                parts.append(empty)
        return jnp.concatenate(parts, axis=1)

    blocks = []
    edges = []
    for c in range(3):
        above = jnp.zeros((8, span), F32)
        below = jnp.zeros((8, span), F32)
        for q in range(4):
            lines = [line(q, c, b) for b in range(3)]
            above = jnp.where((row == q) & (odd == 0), lines[2], above)
            below = jnp.where((row == 4 + q) & (odd == 1), lines[0], below)
            parts = []
            for j in range(4):
                place = 2 * j + odd + 1 - row
                out = jnp.zeros((8, span), F32)
                for b in range(3):
                    out = jnp.where(place == b, lines[b], out)
                parts.append(out)
            blocks.append((q, c, jnp.concatenate(parts, axis=1)))
        zero = jnp.zeros((8, span), F32)
        edges.append(jnp.concatenate([above, zero, zero, below], axis=1))
    blocks.sort(key=lambda item: item[:2])
    rows = [block for _, _, block in blocks] + edges + [jnp.zeros((8, 4 * span), F32)]
    r_ref[...] = jnp.concatenate(rows, axis=0).astype(BF)


def main_kernel(
    whole, vol, cw, cb, rw, out, vbuf, tb, x0, x1, h0, h1, sline, hal, a_ref, r_ref, bias, acc, exst, exin, exdiag,
    prev, following, stats, taken, final, vsem, hsem, lsem, esem, csem, each,
):
    ch, planes, height, width = vol.shape
    pairs = planes // 2
    first = 1
    gap = pairs - first
    count = pairs + 1
    spare = pairs + 1
    windows = height // 2
    groups = height // 8
    n = lax.axis_size("disp")
    me = lax.axis_index("disp")
    r = lax.axis_index("rows")
    up = jnp.minimum(me + 1, n - 1)
    down = jnp.maximum(me - 1, 0)
    xs = (x0, x1)
    hids = (h0, h1)

    def pair_of(item):
        return jnp.where(item <= gap, first + item, item - gap - 1) if not isinstance(item, int) else (
            first + item if item <= gap else item - gap - 1
        )

    def turned(t):
        return (first + t if t < gap else t - gap + 1) if isinstance(t, int) else jnp.where(t < gap, first + t, t - gap + 1)

    def send(src, dst, sems, index, where):
        return pltpu.make_async_remote_copy(
            src_ref=src,
            dst_ref=dst,
            send_sem=sems.at[0, index],
            recv_sem=sems.at[1, index],
            device_id=where,
            device_id_type=MESH,
        )

    def load(p):
        return pltpu.make_async_copy(vol.at[:, p], vbuf.at[p + 1], vsem.at[p])

    def start_pair(t, carry):
        load(2 * turned(t) - 1).start()
        load(2 * turned(t)).start()
        return carry

    lead = min(2, pairs - 1)
    lax.fori_loop(0, lead, start_pair, 0)
    load(planes - 1).start()
    load(0).start()
    fetch = 3
    lax.fori_loop(lead, min(fetch, pairs - 1), start_pair, 0)

    barrier = pltpu.get_barrier_semaphore()
    pl.semaphore_signal(barrier, inc=1, device_id={"rows": 1 - r}, device_id_type=MESH)
    for j in range(1, n):
        pl.semaphore_signal(barrier, inc=1, device_id={"disp": lax.rem(me + j, n)}, device_id_type=MESH)
    for j in (1, n - 1):
        where = {"disp": lax.rem(me + j, n), "rows": 1 - r}
        pl.semaphore_signal(barrier, inc=1, device_id=where, device_id_type=MESH)
    piece = 4
    pieces = ch // piece

    def raw(t):
        rows = pl.ds(t * piece, piece)

        @pl.when(me < n - 1)
        def _():
            send(vol.at[rows, planes - 1], vbuf.at[0, rows], hsem, 0, {"disp": up}).start()

        @pl.when(me > 0)
        def _():
            send(vol.at[rows, 0], vbuf.at[planes + 1, rows], hsem, 1, {"disp": down}).start()


    @pl.when(me == 0)
    def _():
        vbuf[0] = jnp.zeros((ch, height, width), BF)
        hal[0] = jnp.zeros((ch, width), BF)

    @pl.when(me == n - 1)
    def _():
        vbuf[planes + 1] = jnp.zeros((ch, height, width), BF)
        hal[planes + 1] = jnp.zeros((ch, width), BF)

    across = width // LANES
    edge = (height - 1) * (1 - r)

    def turn_part(index, part):
        cols = slice(part * LANES, (part + 1) * LANES)
        tb[index, :, :, cols] = jnp.swapaxes(vbuf[index, :, :, cols], 0, 1)

    def turn(index):
        for part in range(across):
            turn_part(index, part)

    far = {"disp": up, "rows": 1 - r}
    near = {"disp": down, "rows": 1 - r}
    last_line = send(sline.at[planes], hal.at[planes], lsem, pairs, {"rows": 1 - r})
    first_line = send(sline.at[1], hal.at[1], lsem, 0, {"rows": 1 - r})
    last_far = send(sline.at[planes], hal.at[0], lsem, pairs + 1, far)
    first_near = send(sline.at[1], hal.at[planes + 1], lsem, pairs + 2, near)

    def lines(s):
        both = pl.ds(2 * s, 2)
        return send(sline.at[both], hal.at[both], lsem, s, {"rows": 1 - r})

    def keep(t):
        s = turned(t)
        await_pair(s)

        @pl.when(t + fetch < pairs - 1)
        def _():
            start_pair(t + fetch, 0)

        for f in range(2):
            turn(2 * s + f)
            sline[2 * s + f] = tb[2 * s + f, edge]

    def await_pair(s):
        load(2 * s - 1).wait()
        load(2 * s).wait()

    def early(t, carry):
        keep(t)
        return carry

    def late(t, carry):
        keep(t)
        lines(turned(t)).start()

        @pl.when(t % 4 == 1)
        def _():
            raw((t - 1) // 4)

        return carry

    lax.fori_loop(0, lead, early, 0)
    pl.semaphore_wait(barrier, n + 2)

    raw_up = send(vol.at[:, planes - 1], vbuf.at[0], hsem, 0, {"disp": up})
    raw_down = send(vol.at[:, 0], vbuf.at[planes + 1], hsem, 1, {"disp": down})

    for t in range(lead):
        lines(turned(t)).start()
    raw(0)
    fill_a(cw, a_ref)
    fill_r(rw, r_ref)
    one = lax.broadcasted_iota(jnp.int32, (ch, ch), 0) == lax.broadcasted_iota(jnp.int32, (ch, ch), 1)
    column = jnp.sum(jnp.where(one, jnp.broadcast_to(cb[...], (ch, ch)), 0.0), axis=1, keepdims=True)
    bias[...] = jnp.concatenate([jnp.broadcast_to(column, (ch, LANES))] * 4, axis=0)
    acc[...] = jnp.zeros_like(acc)
    h1[...] = jnp.zeros_like(h1)
    load(planes - 1).wait()
    load(0).wait()
    for index in (planes, 1):
        turn(index)
        sline[index] = tb[index, edge]
    last_line.start()
    first_line.start()

    @pl.when(me < n - 1)
    def _():
        last_far.start()

    @pl.when(me > 0)
    def _():
        first_near.start()

    lax.fori_loop(lead, pairs - 1, late, 0)
    for t in range(1 + sum(t % 4 == 1 for t in range(lead, pairs - 1)), pieces):
        raw(t)

    def put_row(x, f, index, line):
        if line == 0:
            value = hal[index]
            value = jnp.where(r == 1, value, jnp.zeros_like(value))
        elif line == height + 1:
            value = hal[index]
            value = jnp.where(r == 0, value, jnp.zeros_like(value))
        else:
            value = tb[index, line - 1]
        at = slice(line * ch, (line + 1) * ch)
        x[f, 0, at, :] = moved(value, 1)
        x[f, 1, at, :] = value
        x[f, 2, at, :] = moved(value, -1)

    def put_rows(x, s, lines_):
        for line in lines_:
            for f in range(2):
                put_row(x, f, 2 * s + f, line)

    def regress(k, hid):
        for g in range(groups):
            span = 16 * ch
            part = jnp.dot(r_ref[...], hid[span * g : span * (g + 1), :], preferred_element_type=F32)

            def gathered(base, step):
                one, two, three = (part[base + step * c : base + step * c + 8] for c in range(3))
                return moved(one, 1) + two + moved(three, -1)

            rows = slice(8 * g, 8 * g + 8)
            for q in range(4):
                acc[2 * k + q, rows, :] += gathered(24 * q, 8)
            beyond = gathered(96, 8)
            if g > 0:
                for q in range(4):
                    acc[2 * k + q, 8 * g - 1 : 8 * g, :] += beyond[q : q + 1]
            if g < groups - 1:
                for q in range(4):
                    acc[2 * k + q, 8 * g + 8 : 8 * g + 9, :] += beyond[4 + q : 5 + q]
            if g == 0:
                exst[k, 0:4, :] = beyond[0:4]
            if g == groups - 1:
                exst[k, 4:8, :] = beyond[4:8]

    def product(low, high, hid, between):
        for j in range(windows):
            rows = slice(2 * j * ch, (2 * j + 4) * ch)
            x = jnp.concatenate([x[f, c, rows, :] for x in (low, high) for f in range(2) for c in range(3)], axis=0)
            pre = jnp.dot(a_ref[...], x, preferred_element_type=F32) + jnp.tile(bias[...], (1, across))
            hid[4 * ch * j : 4 * ch * (j + 1), :] = jnp.maximum(pre, 0.0).astype(BF)
            between(j)

    def extra(k):
        return send(exst.at[k], exin.at[k], esem, k, {"rows": 1 - r})

    cost_up = send(acc.at[planes + 1], prev, csem, 0, {"disp": up})
    cost_down = send(acc.at[0], following, csem, 1, {"disp": down})
    extra_up = send(exst.at[pairs - 1], exdiag.at[0], csem, 2, far)
    extra_down = send(exst.at[0], exdiag.at[1], csem, 3, near)

    def take_after():
        last_line.wait_recv()

        @pl.when(me < n - 1)
        def _():
            first_near.wait_recv()
            raw_down.wait_recv()

        turn(planes + 1)

    def take_before():
        first_line.wait_recv()

        @pl.when(me > 0)
        def _():
            last_far.wait_recv()
            raw_up.wait_recv()

        turn(0)

    for item in range(2):
        if item < gap:
            put_rows(xs[item], pair_of(item), range(1, height + 1))
    for item in range(2):
        if item < gap:
            lines(pair_of(item)).wait_recv()
            put_rows(xs[item], pair_of(item), (0, height + 1))
        else:
            take_after()
            put_rows(xs[item], pair_of(item), range(height + 2))

    def step(i, parity):
        low, high = xs[parity], xs[1 - parity]
        s = pair_of(i + 2)
        s = jnp.where(s > pairs, pairs, s)
        k = jnp.where((i == 0) | (i == gap + 1), spare, pair_of(i - 1))

        @pl.when((s > 0) & (s < pairs) & (i + 2 < count))
        def _():
            lines(s).wait_recv()

        @pl.when(i + 2 == gap)
        def _():
            take_after()

        @pl.when(i + 1 == gap)
        def _():
            take_before()

        def build(j):
            top = height + 2 if j == windows - 1 else 2 * j + 2
            put_rows(low, s, range(2 * j, top))

        def full():
            regress(k, hids[1 - parity])
            product(low, high, hids[parity], build)

        if parity != gap % 2:
            full()
        else:

            @pl.when(i != gap)
            def _():
                full()

            @pl.when(i == gap)
            def _():
                regress(k, hids[1 - parity])
                for j in range(windows):
                    build(j)

        @pl.when(k < pairs)
        def _():
            extra(k).start()

        @pl.when((i == gap) & (me < n - 1))
        def _():
            cost_up.start()
            extra_up.start()

    def two(t, carry):
        step(2 * t, 0)

        @pl.when(2 * t + 1 < count)
        def _():
            step(2 * t + 1, 1)

        return carry

    lax.fori_loop(0, (count + 1) // 2, two, 0)
    regress(first - 1, hids[(count - 1) % 2])
    extra(first - 1).start()

    @pl.when(me > 0)
    def _():
        cost_down.start()
        extra_down.start()

    @pl.when(me < n - 1)
    def _():
        raw_up.wait_send()
        last_far.wait_send()

    @pl.when(me > 0)
    def _():
        raw_down.wait_send()
        first_near.wait_send()

    last_line.wait_send()
    first_line.wait_send()

    def line_sent(s, carry):
        lines(s).wait_send()
        return carry

    lax.fori_loop(1, pairs, line_sent, 0)

    mine = lax.broadcasted_iota(jnp.int32, (height, width), 0) == (1 - r) * (height - 1)

    def add_row(index, value):
        acc[index] += jnp.where(mine, jnp.broadcast_to(value, (height, width)), 0.0)

    def collect(k, carry):
        extra(k).wait()
        for q in range(4):
            add_row(2 * k + q, exin[k, pl.ds(4 * r + q, 1), :])
        return carry

    def collect_end(k):
        extra(k).wait()
        for q in range(4):
            if 1 <= 2 * k + q <= planes:
                add_row(2 * k + q, exin[k, pl.ds(4 * r + q, 1), :])

    lax.fori_loop(first, pairs - 1, collect, 0)
    collect_end(pairs - 1)
    collect_end(0)

    @pl.when(me > 0)
    def _():
        cost_up.wait_recv()
        extra_up.wait_recv()
        acc[1] += prev[...]
        add_row(1, exdiag[0, pl.ds(4 * r + 3, 1), :])

    @pl.when(me < n - 1)
    def _():
        cost_down.wait_recv()
        extra_down.wait_recv()
        acc[planes] += following[...]
        add_row(planes, exdiag[1, pl.ds(4 * r, 1), :])

    for k in range(1, first):
        collect(k, 0)

    low_cost = acc[1]
    for p in range(2, planes + 1):
        low_cost = jnp.minimum(low_cost, acc[p])
    base = (me * planes).astype(F32)
    total = jnp.zeros((height, width), F32)
    moment = jnp.zeros((height, width), F32)
    for p in range(planes):
        expo = jnp.exp(low_cost - acc[p + 1])
        total += expo
        moment += (base + float(p)) * expo
    peak = -low_cost

    @pl.when(me < n - 1)
    def _():
        cost_up.wait_send()
        extra_up.wait_send()

    @pl.when(me > 0)
    def _():
        cost_down.wait_send()
        extra_down.wait_send()

    if not whole:
        out[0] = peak
        out[1] = total
        out[2] = moment
        return

    def place(k):
        at = (k // across) * 8, (k % across) * LANES
        return slice(at[0], at[0] + 8), slice(at[1], at[1] + LANES)

    for k in range(n):
        rows, cols = place(k)
        stats[k, 0] = peak[rows, cols]
        stats[k, 1] = total[rows, cols]
        stats[k, 2] = moment[rows, cols]

    copies = []
    for j in sorted(range(1, n), key=lambda j: -min(j, n - j)):
        peer = lax.rem(me + j, n)
        copies.append(send(stats.at[peer], taken.at[j], each, j, {"disp": peer}))
        copies[-1].start()
    for copy in copies:
        copy.wait_recv()
    sent = copies
    parts = [stats[me]] + [taken[j] for j in range(1, n)]
    top = parts[0][0]
    for part in parts[1:]:
        top = jnp.maximum(top, part[0])
    total = jnp.zeros_like(top)
    moment = jnp.zeros_like(top)
    for part in parts:
        scale = jnp.exp(part[0] - top)
        total += part[1] * scale
        moment += part[2] * scale
    final[me] = moment / total

    copies = []
    for j in sorted(range(1, n), key=lambda j: -min(j, n - j)):
        peer = lax.rem(me + j, n)
        copies.append(send(final.at[me], final.at[me], each, n + j, {"disp": peer}))
        copies[-1].start()
    for copy in copies:
        copy.wait_recv()
    for copy in sent + copies:
        copy.wait_send()
    for k in range(n):
        rows, cols = place(k)
        out[rows, cols] = final[k]


def body(volume, conv_weight, conv_bias, reg_weight):
    ch, planes, height, width = volume.shape
    n = lax.axis_size("disp")
    pairs = planes // 2
    whole = height * width == 8 * LANES * n
    lines = (height + 2) * ch
    slab = pltpu.VMEM((2, 3, lines, width), BF)
    vmem = pl.BlockSpec(memory_space=pltpu.VMEM)
    depth = 48 * ch
    flops = 2 * 4 * ch * depth * width * (height // 2) * pairs
    result = pl.pallas_call(
        functools.partial(main_kernel, whole),
        in_specs=[pl.BlockSpec(memory_space=pl.ANY), vmem, vmem, vmem],
        out_specs=vmem,
        out_shape=jax.ShapeDtypeStruct((height, width) if whole else (3, height, width), F32),
        scratch_shapes=[
            pltpu.VMEM((planes + 2, ch, height, width), BF),
            pltpu.VMEM((planes + 2, height, ch, width), BF),
            slab,
            slab,
            pltpu.VMEM((2 * ch * height, width), BF),
            pltpu.VMEM((2 * ch * height, width), BF),
            pltpu.VMEM((planes + 2, ch, width), BF),
            pltpu.VMEM((planes + 2, ch, width), BF),
            pltpu.VMEM((4 * ch, depth), BF),
            pltpu.VMEM((128, 16 * ch), BF),
            pltpu.VMEM((4 * ch, LANES), F32),
            pltpu.VMEM((planes + 6, height, width), F32),
            pltpu.VMEM((pairs + 2, 8, width), F32),
            pltpu.VMEM((pairs, 8, width), F32),
            pltpu.VMEM((2, 8, width), F32),
            pltpu.VMEM((height, width), F32),
            pltpu.VMEM((height, width), F32),
            pltpu.VMEM((n, 3, 8, LANES), F32),
            pltpu.VMEM((n, 3, 8, LANES), F32),
            pltpu.VMEM((n, 8, LANES), F32),
            pltpu.SemaphoreType.DMA((planes,)),
            pltpu.SemaphoreType.DMA((2, 2)),
            pltpu.SemaphoreType.DMA((2, pairs + 3)),
            pltpu.SemaphoreType.DMA((2, pairs)),
            pltpu.SemaphoreType.DMA((2, 4)),
            pltpu.SemaphoreType.DMA((2, 2 * n)),
        ],
        compiler_params=pltpu.CompilerParams(collective_id=0, has_side_effects=True, vmem_limit_bytes=56 << 20),
        cost_estimate=pl.CostEstimate(flops=flops, bytes_accessed=2 * volume.size, transcendentals=0),
        name="fused",
    )(volume, conv_weight, conv_bias[None, :], reg_weight)
    if whole:
        return result
    value = joined(result, "disp")
    return value[2] / value[1]


def solution(mesh):
    in_specs = (P(None, "disp", ("tiles", "rows"), None), P(), P(), P())
    out_specs = P(("tiles", "rows"), None)
    return jax.shard_map(body, mesh=mesh, in_specs=in_specs, out_specs=out_specs, check_vma=False)
```
